32 devices in a mesh: fsdp: 2 (over x), ctx: 4 (over y, core), tp: 4 (over z).
Axes of the slice: x: 2, y: 2, z: 4, core: 2. Of those that a mesh axis runs over, the one named last changes fastest.
Arguments:
- block_input: bfloat16 [2, 2048, 1024], P('fsdp', 'ctx'), may hold values from -6 to 6
- segment_ids: int32 [2, 2048], P('fsdp'), may hold values from 0 to 3, as said below
- positions: int32 [2, 2048], P('fsdp', 'ctx'), may hold values from 0 to 1023, as said below
- attn_gain: bfloat16 [1024], P('fsdp'), may hold values from 0.5 to 1.5
- query_weight: bfloat16 [1024, 1024], P('fsdp', 'tp'), may hold values from -0.1875 to 0.1875
- key_matrix: bfloat16 [1024, 512], P('fsdp', 'tp'), may hold values from -0.1875 to 0.1875
- value_matrix: bfloat16 [1024, 512], P('fsdp', 'tp'), may hold values from -0.1875 to 0.1875
- output_weight: bfloat16 [1024, 1024], P('fsdp', 'tp'), may hold values from -0.75 to 0.75
- query_gain: bfloat16 [64], replicated, may hold values from 0.5 to 1.5
- key_gain: bfloat16 [64], replicated, may hold values from 0.5 to 1.5
- ffn_gain: bfloat16 [1024], P('fsdp'), may hold values from 0.5 to 1.5
- gate_weight: bfloat16 [1024, 4608], P('fsdp', 'tp'), may hold values from -0.1875 to 0.1875
- up_weight: bfloat16 [1024, 4608], P('fsdp', 'tp'), may hold values from -0.1875 to 0.1875
- down_weight: bfloat16 [1024, 4608], P('fsdp', 'tp'), may hold values from -0.09375 to 0.09375
- out_grad: bfloat16 [2, 2048, 1024], P('fsdp', 'ctx'), may hold values from -6 to 6
Outputs:
- block_output: bfloat16 [2, 2048, 1024], P('fsdp', 'ctx')
- input_grad: float32 [2, 2048, 1024], P('fsdp', 'ctx')
- attn_gain_grad: float32 [1024], P('fsdp')
- query_weight_grad: float32 [1024, 1024], P('fsdp', 'tp')
- key_weight_grad: float32 [1024, 512], P('fsdp', 'tp')
- value_weight_grad: float32 [1024, 512], P('fsdp', 'tp')
- output_weight_grad: float32 [1024, 1024], P('fsdp', 'tp')
- query_gain_grad: float32 [64], replicated
- key_gain_grad: float32 [64], replicated
- ffn_gain_grad: float32 [1024], P('fsdp')
- gate_weight_grad: float32 [1024, 4608], P('fsdp', 'tp')
- up_weight_grad: float32 [1024, 4608], P('fsdp', 'tp')
- down_weight_grad: float32 [1024, 4608], P('fsdp', 'tp')
The draws below stay inside these ranges and needn't reach their ends.
Inputs may be any that keep to these rules, and one draw needn't show every extreme that they name: `segment_ids`: segment ids never fall along a sequence, and each of its 4 documents holds at least one token. positions start at 0 on each document's first token and rise by one along the document; in every sequence one document holds exactly 1024 tokens and the others fewer.
All inputs are finite; a program needn't handle non-finite values.
Results may differ from the reference program's by a relative error of at most 0.02.
Values may be sent and summed in bfloat16 or wider, within the bound.
A program may use at most 128 MiB of HBM per device.

```python
import jax
import jax.numpy as jnp
from jax import lax

MODEL_WIDTH = 1024
QUERY_HEADS = 16
KEY_VALUE_HEADS = 8
HEAD_SIZE = 64
FEEDFORWARD_UNITS = 4608
SEQ_LEN = 2048
DOCS = 4
SEQS = 2


def segment_layout(key):
    keys = jax.random.split(jax.random.fold_in(key, 7), SEQS)
    longest = SEQ_LEN // 2
    remain = SEQ_LEN - longest

    def one(sub):
        first_key, second_key = jax.random.split(sub)
        small_cuts = jnp.sort(jax.random.permutation(first_key, remain - 1)[:DOCS - 2] + 1).astype(jnp.int32)
        bounds = jnp.concatenate([jnp.zeros((1,), jnp.int32), small_cuts, jnp.full((1,), remain, jnp.int32)])
        small = (bounds[1:] - bounds[:-1]).astype(jnp.int32)
        chosen = jax.random.randint(second_key, (), 0, DOCS).astype(jnp.int32)
        slot = jnp.arange(DOCS, dtype=jnp.int32)
        source = jnp.clip(slot - (slot > chosen).astype(jnp.int32), 0, DOCS - 2)
        lengths = jnp.where(slot == chosen, longest, small[source]).astype(jnp.int32)
        ends = jnp.cumsum(lengths).astype(jnp.int32)
        starts = (ends - lengths).astype(jnp.int32)
        index = jnp.arange(SEQ_LEN, dtype=jnp.int32)
        ids = jnp.sum((index[:, None] >= ends[None, :DOCS - 1]).astype(jnp.int32), axis=1).astype(jnp.int32)
        first = jnp.sum(jnp.where(ids[:, None] == slot[None, :], starts[None, :], 0), axis=1).astype(jnp.int32)
        return (ids, index - first)
    return jax.vmap(one)(keys)


def draw_segment_ids(key, part):
    return segment_layout(key)[0]


def draw_positions(key, part):
    return segment_layout(key)[1]


def shard_levels(key, extent, cuts, least, largest):
    level, own = 1.0, jax.random.fold_in(key, 6)
    for axis_at, parts in cuts:
        steps = jnp.exp(jax.random.uniform(jax.random.fold_in(own, axis_at), (parts,), jnp.float32, least / len(cuts), largest / len(cuts)))
        level = level * jnp.repeat(steps, extent[axis_at] // parts).reshape([-1 if axis == axis_at else 1 for axis in range(len(extent))])
    return level


def gaussian(rng, extent, deviation, reach, pieces=(), kind=jnp.bfloat16):
    array = deviation * jax.random.normal(rng, extent, jnp.float32)
    if pieces:
        array = array * shard_levels(rng, extent, pieces, -0.22, 0.18)
    return jnp.clip(array, -reach, reach).astype(kind)


def setup_inputs(seed: int = 0) -> dict:
    key_list = jax.random.split(jax.random.key(seed), 16)
    return {
        "block_input": gaussian(key_list[0], (SEQS, SEQ_LEN, MODEL_WIDTH), 1.0, 6.0, ((0, 2), (1, 4))),
        "segment_ids": draw_segment_ids(jax.random.fold_in(key_list[15], 71), 0),
        "positions": draw_positions(jax.random.fold_in(key_list[15], 71), 0),
        "attn_gain": jnp.clip(1.0 + 0.1 * jax.random.normal(key_list[3], (MODEL_WIDTH,), jnp.float32), 0.5, 1.5).astype(jnp.bfloat16),
        "query_weight": gaussian(key_list[4], (MODEL_WIDTH, QUERY_HEADS * HEAD_SIZE), MODEL_WIDTH ** -0.5, 0.1875, ((0, 2), (1, 4))),
        "key_matrix": gaussian(key_list[5], (MODEL_WIDTH, KEY_VALUE_HEADS * HEAD_SIZE), MODEL_WIDTH ** -0.5, 0.1875, ((0, 2), (1, 4))),
        "value_matrix": gaussian(key_list[6], (MODEL_WIDTH, KEY_VALUE_HEADS * HEAD_SIZE), MODEL_WIDTH ** -0.5, 0.1875, ((0, 2), (1, 4))),
        "output_weight": gaussian(key_list[7], (MODEL_WIDTH, QUERY_HEADS * HEAD_SIZE), (QUERY_HEADS * HEAD_SIZE // 16) ** -0.5, 0.75, ((0, 2), (1, 4))),
        "query_gain": jnp.clip(1.0 + 0.1 * jax.random.normal(key_list[8], (HEAD_SIZE,), jnp.float32), 0.5, 1.5).astype(jnp.bfloat16),
        "key_gain": jnp.clip(1.0 + 0.1 * jax.random.normal(key_list[9], (HEAD_SIZE,), jnp.float32), 0.5, 1.5).astype(jnp.bfloat16),
        "ffn_gain": jnp.clip(1.0 + 0.1 * jax.random.normal(key_list[10], (MODEL_WIDTH,), jnp.float32), 0.5, 1.5).astype(jnp.bfloat16),
        "gate_weight": gaussian(key_list[11], (MODEL_WIDTH, FEEDFORWARD_UNITS), MODEL_WIDTH ** -0.5, 0.1875, ((0, 2), (1, 4))),
        "up_weight": gaussian(key_list[12], (MODEL_WIDTH, FEEDFORWARD_UNITS), MODEL_WIDTH ** -0.5, 0.1875, ((0, 2), (1, 4))),
        "down_weight": gaussian(key_list[13], (MODEL_WIDTH, FEEDFORWARD_UNITS), FEEDFORWARD_UNITS ** -0.5, 0.09375, ((0, 2), (1, 4))),
        "out_grad": gaussian(key_list[14], (SEQS, SEQ_LEN, MODEL_WIDTH), 1.0, 6.0, ((0, 2), (1, 4))),
    }


eps = 1e-05
theta = 1000000.0

def rms_scale(value_rows):
    return lax.rsqrt(lax.optimization_barrier(jnp.mean(value_rows * value_rows, axis=-1, keepdims=True)) + eps)

def norm_back(value_rows, scale, gain, grad_out):
    normed = value_rows * scale
    grad_normed = grad_out * gain
    grad_values = scale * (grad_normed - normed * lax.optimization_barrier(jnp.mean(grad_normed * normed, axis=-1, keepdims=True)))
    return (grad_values, grad_out * normed)

def rope_tables(positions, width):
    half = width // 2
    freq = theta ** (-(jnp.arange(half, dtype=jnp.float32) * 2.0 / width))
    angle = positions.astype(jnp.float32)[:, None] * freq[None, :]
    angle = jnp.concatenate([angle, angle], axis=-1)
    return (jnp.cos(angle)[:, None, :], jnp.sin(angle)[:, None, :])

def rotate(value_rows, cosine, sine):
    half = value_rows.shape[-1] // 2
    turned = jnp.concatenate([-value_rows[..., half:], value_rows[..., :half]], axis=-1)
    return value_rows * cosine + turned * sine

def rotate_back(grads, cosine, sine):
    half = grads.shape[-1] // 2
    scaled = grads * sine
    turned = jnp.concatenate([scaled[..., half:], -scaled[..., :half]], axis=-1)
    return grads * cosine + turned

def block_scores(query_block, keys, mask):
    groups = query_block.shape[1] // keys.shape[1]
    grouped = query_block.reshape(query_block.shape[0], keys.shape[1], groups, query_block.shape[2])
    scores = jnp.einsum('bkgd,skd->kgbs', grouped.astype(jnp.float32), keys.astype(jnp.float32)) * query_block.shape[2] ** (-0.5)
    return (jnp.where(mask[None, None], scores, -1e+30), grouped)

def attend_block(query_block, keys, value_rows, mask):
    scores, grouped = block_scores(query_block, keys, mask)
    top = lax.optimization_barrier(jnp.max(scores, axis=-1, keepdims=True))
    total = lax.optimization_barrier(jnp.sum(jnp.exp(scores - top), axis=-1, keepdims=True))
    lse = top + jnp.log(total)
    probs = jnp.exp(scores - lse).astype(jnp.bfloat16)
    out = jnp.einsum('kgbs,skd->bkgd', probs.astype(jnp.float32), value_rows.astype(jnp.float32))
    return (out.reshape(query_block.shape[0], -1).astype(jnp.bfloat16), lse[..., 0])

def attend_block_back(query_block, keys, value_rows, out_block, grad_block, lse, mask):
    scores, grouped = block_scores(query_block, keys, mask)
    probs = jnp.exp(scores - lse[..., None])
    shape = grouped.shape
    grad_grouped = grad_block.reshape(shape).astype(jnp.float32)
    out_grouped = out_block.reshape(shape).astype(jnp.float32)
    grad_values = jnp.einsum('kgbs,bkgd->skd', probs.astype(jnp.bfloat16).astype(jnp.float32), grad_grouped)
    grad_probs = jnp.einsum('bkgd,skd->kgbs', grad_grouped, value_rows.astype(jnp.float32))
    delta = jnp.transpose(lax.optimization_barrier(jnp.sum(grad_grouped * out_grouped, axis=-1)), (1, 2, 0))[..., None]
    grad_scores = (probs * (grad_probs - delta)).astype(jnp.bfloat16).astype(jnp.float32)
    factor = shape[3] ** (-0.5)
    grad_query = jnp.einsum('kgbs,skd->bkgd', grad_scores, keys.astype(jnp.float32)) * factor
    grad_keys = jnp.einsum('kgbs,bkgd->skd', grad_scores, grouped.astype(jnp.float32)) * factor
    return (grad_query.reshape(query_block.shape), grad_keys, grad_values)

def reference(block_input, segment_ids, positions, attn_gain, query_weight, key_matrix, value_matrix, output_weight, query_gain, key_gain, ffn_gain, gate_weight, up_weight, down_weight, out_grad):
    single_float = jnp.float32
    brain_float_half = jnp.bfloat16
    span_length = SEQ_LEN
    block = min(512, span_length)
    count = span_length // block
    gain_one = attn_gain.astype(single_float)
    gain_two = ffn_gain.astype(single_float)
    query_gain_f = query_gain.astype(single_float)
    key_gain_f = key_gain.astype(single_float)
    key_index = jnp.arange(span_length, dtype=jnp.int32)

    def one(carry, items):
        inputs, seg_all, pos, grad_out = items
        inputs_f = inputs.astype(single_float)
        cosine, sine = rope_tables(pos, HEAD_SIZE)
        scale_one = rms_scale(inputs_f)
        first_normalized = (inputs_f * scale_one * gain_one).astype(brain_float_half)
        query_raw = jnp.dot(first_normalized, query_weight, preferred_element_type=single_float).reshape(span_length, QUERY_HEADS, HEAD_SIZE)
        key_unrotated = jnp.dot(first_normalized, key_matrix, preferred_element_type=single_float).reshape(span_length, KEY_VALUE_HEADS, HEAD_SIZE)
        value_rows = jnp.dot(first_normalized, value_matrix, preferred_element_type=single_float).astype(brain_float_half).reshape(span_length, KEY_VALUE_HEADS, HEAD_SIZE)
        query_scale = rms_scale(query_raw)
        key_scale = rms_scale(key_unrotated)
        query_bf = rotate(query_raw * query_scale * query_gain_f, cosine, sine).astype(brain_float_half)
        key_bf = rotate(key_unrotated * key_scale * key_gain_f, cosine, sine).astype(brain_float_half)

        def block_mask(index):
            q_pos = lax.dynamic_slice_in_dim(key_index, index * block, block)
            q_seg = lax.dynamic_slice_in_dim(seg_all, index * block, block)
            return (q_seg[:, None] == seg_all[None, :]) & (key_index[None, :] <= q_pos[:, None])

        def forward_block(index):
            query_block = lax.dynamic_slice_in_dim(query_bf, index * block, block)
            return attend_block(query_block, key_bf, value_rows, block_mask(index))
        heads_blocks, lse_blocks = lax.map(forward_block, jnp.arange(count, dtype=jnp.int32))
        heads_out = heads_blocks.reshape(span_length, QUERY_HEADS * HEAD_SIZE)
        residual = inputs_f + jnp.dot(heads_out, output_weight.T, preferred_element_type=single_float)
        scale_two = rms_scale(residual)
        normed_two = (residual * scale_two * gain_two).astype(brain_float_half)
        gate = jnp.dot(normed_two, gate_weight, preferred_element_type=single_float)
        up = jnp.dot(normed_two, up_weight, preferred_element_type=single_float)
        sigmoid = jax.nn.sigmoid(gate)
        silu_gate = gate * sigmoid
        activation = (silu_gate * up).astype(brain_float_half)
        output = (residual + jnp.dot(activation, down_weight.T, preferred_element_type=single_float)).astype(brain_float_half)
        down_grad = jnp.dot(grad_out.T, activation, preferred_element_type=single_float)
        grad_act = jnp.dot(grad_out, down_weight, preferred_element_type=single_float)
        grad_gate = (grad_act * up * sigmoid * (1.0 + gate * (1.0 - sigmoid))).astype(brain_float_half)
        grad_up = (grad_act * silu_gate).astype(brain_float_half)
        gate_grad = jnp.dot(normed_two.T, grad_gate, preferred_element_type=single_float)
        up_grad = jnp.dot(normed_two.T, grad_up, preferred_element_type=single_float)
        normed_two_grad = jnp.dot(grad_gate, gate_weight.T, preferred_element_type=single_float) + jnp.dot(grad_up, up_weight.T, preferred_element_type=single_float)
        residual_back, ffn_terms = norm_back(residual, scale_two, gain_two, normed_two_grad)
        residual_grad = grad_out.astype(single_float) + residual_back
        residual_bf = residual_grad.astype(brain_float_half)
        out_weight_grad = jnp.dot(residual_bf.T, heads_out, preferred_element_type=single_float)
        heads_grad = jnp.dot(residual_bf, output_weight, preferred_element_type=single_float).astype(brain_float_half)

        def backward_block(acc, index):
            query_block = lax.dynamic_slice_in_dim(query_bf, index * block, block)
            out_block = lax.dynamic_slice_in_dim(heads_out, index * block, block)
            grad_block = lax.dynamic_slice_in_dim(heads_grad, index * block, block)
            grad_query, grad_keys, grad_values = attend_block_back(query_block, key_bf, value_rows, out_block, grad_block, lse_blocks[index], block_mask(index))
            return ((acc[0] + grad_keys, acc[1] + grad_values), grad_query)
        blank_array = jnp.zeros((span_length, KEY_VALUE_HEADS, HEAD_SIZE), single_float)
        (keys_grad_rot, values_grad), query_blocks = lax.scan(backward_block, (blank_array, blank_array), jnp.arange(count, dtype=jnp.int32))
        query_grad_rot = query_blocks.reshape(span_length, QUERY_HEADS, HEAD_SIZE)
        query_pre, query_terms = norm_back(query_raw, query_scale, query_gain_f, rotate_back(query_grad_rot, cosine, sine))
        key_pre, key_terms = norm_back(key_unrotated, key_scale, key_gain_f, rotate_back(keys_grad_rot, cosine, sine))
        query_pre_bf = query_pre.reshape(span_length, -1).astype(brain_float_half)
        key_pre_bf = key_pre.reshape(span_length, -1).astype(brain_float_half)
        values_bf = values_grad.reshape(span_length, -1).astype(brain_float_half)
        q_weight_grad = jnp.dot(first_normalized.T, query_pre_bf, preferred_element_type=single_float)
        k_weight_grad = jnp.dot(first_normalized.T, key_pre_bf, preferred_element_type=single_float)
        v_weight_grad = jnp.dot(first_normalized.T, values_bf, preferred_element_type=single_float)
        normed_one_grad = jnp.dot(query_pre_bf, query_weight.T, preferred_element_type=single_float) + jnp.dot(key_pre_bf, key_matrix.T, preferred_element_type=single_float) + jnp.dot(values_bf, value_matrix.T, preferred_element_type=single_float)
        input_back, attn_terms = norm_back(inputs_f, scale_one, gain_one, normed_one_grad)
        input_grad = residual_grad + input_back
        update = (lax.optimization_barrier(jnp.sum(attn_terms, axis=0)), q_weight_grad, k_weight_grad, v_weight_grad, out_weight_grad, lax.optimization_barrier(jnp.sum(query_terms, axis=(0, 1))), lax.optimization_barrier(jnp.sum(key_terms, axis=(0, 1))), lax.optimization_barrier(jnp.sum(ffn_terms, axis=0)), gate_grad, up_grad, down_grad)
        carry = tuple((old + new for old, new in zip(carry, update)))
        return (carry, (output, input_grad))
    initial_setup = (jnp.zeros((MODEL_WIDTH,), single_float), jnp.zeros((MODEL_WIDTH, QUERY_HEADS * HEAD_SIZE), single_float), jnp.zeros((MODEL_WIDTH, KEY_VALUE_HEADS * HEAD_SIZE), single_float), jnp.zeros((MODEL_WIDTH, KEY_VALUE_HEADS * HEAD_SIZE), single_float), jnp.zeros((MODEL_WIDTH, QUERY_HEADS * HEAD_SIZE), single_float), jnp.zeros((HEAD_SIZE,), single_float), jnp.zeros((HEAD_SIZE,), single_float), jnp.zeros((MODEL_WIDTH,), single_float), jnp.zeros((MODEL_WIDTH, FEEDFORWARD_UNITS), single_float), jnp.zeros((MODEL_WIDTH, FEEDFORWARD_UNITS), single_float), jnp.zeros((MODEL_WIDTH, FEEDFORWARD_UNITS), single_float))
    grads, (outputs, input_grads) = lax.scan(one, initial_setup, (block_input, segment_ids, positions, out_grad))
    return (outputs, input_grads, grads[0], grads[1], grads[2], grads[3], grads[4], grads[5], grads[6], grads[7], grads[8], grads[9], grads[10])
```

```python
import jax
import jax.numpy as jnp
from jax import lax
from jax.sharding import PartitionSpec as P

HEAD_SIZE = 64
MAX_DOC = 1024


eps = 1e-05
theta = 1000000.0


def ring(count, step):
    return [(i, (i + step) % count) for i in range(count)]


def swap(count):
    return [(i, i ^ 1) for i in range(count)]


def rounded(value):
    return lax.reduce_precision(value, 8, 7).astype(jnp.bfloat16)


def take(value, start, size, axis=0):
    return lax.dynamic_slice_in_dim(value, start, size, axis)


def put(whole, part, start, axis=0):
    return lax.dynamic_update_slice_in_dim(whole, part, start, axis)


def gather(part, name, axis=0):
    count, me, size = lax.axis_size(name), lax.axis_index(name), part.shape[axis]
    shape = list(part.shape)
    shape[axis] = count * size
    whole = put(jnp.zeros(shape, part.dtype), part, me * size, axis)
    for k in range(1, count):
        got = lax.ppermute(part, name, ring(count, k))
        whole = put(whole, got, ((me - k) % count) * size, axis)
    return whole


def paired(count):
    return count % 2 == 0


def gather_shared(part):
    ctx = lax.axis_size("ctx")
    size = part.shape[0]
    if not paired(ctx) or size % 32:
        return gather(part, "fsdp")
    count, me = lax.axis_size("fsdp"), lax.axis_index("fsdp")
    half, side = size // 2, lax.axis_index("ctx") % 2
    mine = take(part, side * half, half)
    whole = put(jnp.zeros((count * size, part.shape[1]), part.dtype), part, me * size)
    for k in range(1, count):
        got = lax.ppermute(mine, "fsdp", ring(count, k))
        other = lax.ppermute(got, "ctx", swap(ctx))
        start = ((me - k) % count) * size
        whole = put(whole, got, start + side * half)
        whole = put(whole, other, start + (1 - side) * half)
    return whole


def scatter_rows(part, name):
    count, me = lax.axis_size(name), lax.axis_index(name)
    size = part.shape[0] // count
    total = take(part, me * size, size).astype(jnp.float32)
    for k in range(1, count):
        block = take(part, ((me + k) % count) * size, size)
        total = total + lax.ppermute(block, name, ring(count, k)).astype(jnp.float32)
    return total


def reduce_grad(grad):
    count, me = lax.axis_size("fsdp"), lax.axis_index("fsdp")
    ctx, place = lax.axis_size("ctx"), lax.axis_index("ctx")
    width = grad.shape[1]
    size = grad.shape[0] // count
    split = 2 if paired(ctx) and size % 32 == 0 else 1
    half, side = size // split, place % split
    blocks = grad.reshape(count, split, half, width)
    mine = take(blocks, side, 1, 1)[:, 0]
    if split == 2:
        away = take(blocks, 1 - side, 1, 1)[:, 0]
        got = lax.ppermute(away, "ctx", swap(ctx))
        mine = (mine.astype(jnp.float32) + got.astype(jnp.float32)).astype(jnp.bfloat16)
    total = take(mine, me, 1)[0].astype(jnp.float32)
    for k in range(1, count):
        block = take(mine, (me + k) % count, 1)[0]
        total = total + lax.ppermute(block, "fsdp", ring(count, k)).astype(jnp.float32)
    far = ctx // split
    if far > 1:
        sent = rounded(total)
        if far == 2:
            got = lax.ppermute(sent, "ctx", ring(ctx, split))
            total = sent.astype(jnp.float32) + got.astype(jnp.float32)
        else:
            whole = put(jnp.zeros((far, half, width), jnp.bfloat16), sent[None], place // split)
            for k in range(1, far):
                got = lax.ppermute(sent, "ctx", ring(ctx, k * split))
                whole = put(whole, got[None], (place // split - k) % far)
            total = jnp.sum(whole.astype(jnp.float32), axis=0)
    if split == 1:
        return total
    sent = rounded(total)
    got = lax.ppermute(sent, "ctx", swap(ctx))
    low = jnp.where(side == 0, sent, got)
    high = jnp.where(side == 0, got, sent)
    return jnp.concatenate([low, high], axis=0).astype(jnp.float32)


def dot(left, right, dims=((1,), (0,)), out=jnp.float32):
    return lax.dot_general(left, right, (dims, ((), ())), preferred_element_type=jnp.float32).astype(out)


def rms_scale(value_rows):
    return lax.rsqrt(jnp.mean(value_rows * value_rows, axis=-1, keepdims=True) + eps)


def norm_back(value_rows, scale, gain, grad_out):
    normed = value_rows * scale
    grad_normed = grad_out * gain
    grad_values = scale * (
        grad_normed - normed * jnp.mean(grad_normed * normed, axis=-1, keepdims=True)
    )
    return (grad_values, grad_out * normed)


def rope_tables(positions, width):
    half = width // 2
    freq = theta ** (-(jnp.arange(half, dtype=jnp.float32) * 2.0 / width))
    angle = positions.astype(jnp.float32)[:, None] * freq[None, :]
    angle = jnp.concatenate([angle, angle], axis=-1)
    return (jnp.cos(angle)[:, None, :], jnp.sin(angle)[:, None, :])


def rotate(value_rows, cosine, sine):
    half = value_rows.shape[-1] // 2
    turned = jnp.concatenate([-value_rows[..., half:], value_rows[..., :half]], axis=-1)
    return value_rows * cosine + turned * sine


def rotate_back(grads, cosine, sine):
    half = grads.shape[-1] // 2
    scaled = grads * sine
    turned = jnp.concatenate([scaled[..., half:], -scaled[..., :half]], axis=-1)
    return grads * cosine + turned


def per_device(
    block_input,
    segment_ids,
    positions,
    attn_gain,
    query_weight,
    key_matrix,
    value_matrix,
    output_weight,
    query_gain,
    key_gain,
    ffn_gain,
    gate_weight,
    up_weight,
    down_weight,
    out_grad,
):
    f32 = jnp.float32
    bf16 = jnp.bfloat16
    inputs = block_input[0]
    grad_out = out_grad[0]
    rows = inputs.shape[0]
    width = inputs.shape[1]
    seg_all = segment_ids[0]
    ctx, place = lax.axis_size("ctx"), lax.axis_index("ctx")
    tp, rank = lax.axis_size("tp"), lax.axis_index("tp")
    own = rows // tp
    q_cols, kv_cols = query_weight.shape[1], key_matrix.shape[1]
    q_count, kv_count = q_cols // HEAD_SIZE, kv_cols // HEAD_SIZE
    groups = q_count // kv_count

    gains = gather(jnp.stack([attn_gain, ffn_gain]), "fsdp", 1).astype(f32)
    gain_one, gain_two = gains[0], gains[1]
    w_attn = gather(
        jnp.concatenate([query_weight, key_matrix, value_matrix, output_weight], axis=1), "fsdp"
    )
    w_in, w_out = w_attn[:, : q_cols + 2 * kv_cols], w_attn[:, q_cols + 2 * kv_cols :]
    w_gate = gather_shared(gate_weight)
    w_up = gather_shared(up_weight)
    w_down = gather_shared(down_weight)

    inputs_f = inputs.astype(f32)
    scale_one = rms_scale(inputs_f)
    normed_one = (inputs_f * scale_one * gain_one).astype(bf16)
    cosine, sine = rope_tables(positions[0], HEAD_SIZE)
    mixed = dot(normed_one, w_in)
    query_raw = mixed[:, :q_cols].reshape(rows, q_count, HEAD_SIZE)
    key_raw = mixed[:, q_cols : q_cols + kv_cols].reshape(rows, kv_count, HEAD_SIZE)
    values = mixed[:, q_cols + kv_cols :].astype(bf16)
    query_gain_f = query_gain.astype(f32)
    key_gain_f = key_gain.astype(f32)
    query_scale = rms_scale(query_raw)
    key_scale = rms_scale(key_raw)
    factor = HEAD_SIZE ** (-0.5)
    query = rotate(query_raw * query_scale * query_gain_f, cosine, sine).astype(bf16)
    query = (query * factor).astype(bf16).reshape(rows, kv_count, groups, HEAD_SIZE)
    key = rotate(key_raw * key_scale * key_gain_f, cosine, sine).astype(bf16)
    both = jnp.concatenate([key.reshape(rows, kv_cols), values], axis=1)

    near = min(ctx, 1 + (MAX_DOC - 1 + rows - 1) // rows)
    both_parts, seg_parts, index_parts = [both], [], []
    step = jnp.arange(rows, dtype=jnp.int32)
    for k in range(near):
        if k:
            both_parts.append(lax.ppermute(both, "ctx", ring(ctx, k)))
        start = ((place - k) % ctx) * rows
        seg_parts.append(take(seg_all, start, rows))
        index_parts.append(start + step)
    both_near = jnp.concatenate(both_parts, axis=0)
    seg_near = jnp.concatenate(seg_parts)
    index_near = jnp.concatenate(index_parts)
    mask = (seg_parts[0][:, None] == seg_near[None, :]) & (
        index_near[None, :] <= index_parts[0][:, None]
    )
    keys_near = both_near[:, :kv_cols].reshape(-1, kv_count, HEAD_SIZE)
    values_near = both_near[:, kv_cols:].reshape(-1, kv_count, HEAD_SIZE)

    scores = jnp.einsum("bkgd,skd->kgbs", query, keys_near, preferred_element_type=f32)
    scores = jnp.where(mask[None, None], scores, -1e30)
    top = jnp.max(scores, axis=-1, keepdims=True)
    total = jnp.sum(jnp.exp(scores - top), axis=-1, keepdims=True)
    probs = jnp.exp(scores - (top + jnp.log(total))).astype(bf16)
    heads_out = jnp.einsum("kgbs,skd->bkgd", probs, values_near, preferred_element_type=f32)
    heads_out = heads_out.astype(bf16)
    heads_rows = heads_out.reshape(rows, q_cols)

    def own_rows(value):
        return take(value, rank * own, own)

    attn_part = dot(heads_rows, w_out, ((1,), (1,)), bf16)
    residual = own_rows(inputs).astype(f32) + scatter_rows(attn_part, "tp")
    scale_two = rms_scale(residual)
    normed_two = gather((residual * scale_two * gain_two).astype(bf16), "tp")
    gate = dot(normed_two, w_gate)
    up = dot(normed_two, w_up)
    grad_act = dot(grad_out, w_down)
    sigmoid = jax.nn.sigmoid(gate)
    silu_gate = gate * sigmoid
    activation = (silu_gate * up).astype(bf16)
    grad_gate = (grad_act * up * sigmoid * (1.0 + gate * (1.0 - sigmoid))).astype(bf16)
    grad_up = (grad_act * silu_gate).astype(bf16)

    normed_two_part = (
        dot(grad_gate, w_gate, ((1,), (1,))) + dot(grad_up, w_up, ((1,), (1,)))
    ).astype(bf16)
    normed_two_grad = scatter_rows(normed_two_part, "tp")
    residual_back, ffn_terms = norm_back(residual, scale_two, gain_two, normed_two_grad)
    residual_grad = own_rows(grad_out).astype(f32) + residual_back
    residual_bf = gather(residual_grad.astype(bf16), "tp")

    ffn_part = dot(activation, w_down, ((1,), (1,)), bf16)
    output = gather((residual + scatter_rows(ffn_part, "tp")).astype(bf16), "tp")
    down_grad = reduce_grad(dot(grad_out, activation, ((0,), (0,)), bf16))
    gate_grad = reduce_grad(dot(normed_two, grad_gate, ((0,), (0,)), bf16))
    up_grad = reduce_grad(dot(normed_two, grad_up, ((0,), (0,)), bf16))

    heads_grad = dot(residual_bf, w_out, ((1,), (0,)), bf16)
    out_weight_grad = reduce_grad(dot(residual_bf, heads_rows, ((0,), (0,)), bf16))
    heads_grad = heads_grad.reshape(heads_out.shape)
    values_grad_near = jnp.einsum("kgbs,bkgd->skd", probs, heads_grad, preferred_element_type=f32)
    grad_probs = jnp.einsum("bkgd,skd->kgbs", heads_grad, values_near, preferred_element_type=f32)
    delta = jnp.sum(heads_grad.astype(f32) * heads_out.astype(f32), axis=-1)
    delta = jnp.transpose(delta, (1, 2, 0))[..., None]
    grad_scores = (probs.astype(f32) * (grad_probs - delta)).astype(bf16)
    keys_grad_near = jnp.einsum("kgbs,bkgd->skd", grad_scores, query, preferred_element_type=f32)
    query_grad = (
        jnp.einsum("kgbs,skd->bkgd", grad_scores, keys_near, preferred_element_type=f32) * factor
    )

    both_grad = jnp.concatenate(
        [keys_grad_near.reshape(-1, kv_cols), values_grad_near.reshape(-1, kv_cols)], axis=1
    )
    both_sum = both_grad[:rows]
    for k in range(1, near):
        block = both_grad[k * rows : (k + 1) * rows].astype(bf16)
        both_sum = both_sum + lax.ppermute(block, "ctx", ring(ctx, -k)).astype(f32)
    keys_grad = both_sum[:, :kv_cols].reshape(rows, kv_count, HEAD_SIZE)
    values_bf = both_sum[:, kv_cols:].astype(bf16)

    query_pre, query_terms = norm_back(
        query_raw,
        query_scale,
        query_gain_f,
        rotate_back(query_grad.reshape(query_raw.shape), cosine, sine),
    )
    key_pre, key_terms = norm_back(
        key_raw, key_scale, key_gain_f, rotate_back(keys_grad, cosine, sine)
    )
    mixed_pre = jnp.concatenate(
        [
            query_pre.reshape(rows, q_cols).astype(bf16),
            key_pre.reshape(rows, kv_cols).astype(bf16),
            values_bf,
        ],
        axis=1,
    )
    normed_one_part = dot(mixed_pre, w_in, ((1,), (1,)), bf16)
    normed_one_grad = scatter_rows(normed_one_part, "tp")
    input_back, attn_terms = norm_back(
        own_rows(inputs).astype(f32), own_rows(scale_one), gain_one, normed_one_grad
    )
    input_grad = gather(rounded(residual_grad + input_back), "tp").astype(f32)
    mixed_grad = reduce_grad(dot(normed_one, mixed_pre, ((0,), (0,)), bf16))

    small = lax.psum(
        jnp.concatenate(
            [
                jnp.sum(attn_terms, axis=0),
                jnp.sum(ffn_terms, axis=0),
                jnp.sum(query_terms, axis=(0, 1)),
                jnp.sum(key_terms, axis=(0, 1)),
            ]
        ),
        ("fsdp", "ctx", "tp"),
    )
    share = attn_gain.shape[0]
    first = lax.axis_index("fsdp") * share
    return (
        output[None],
        input_grad[None],
        take(small, first, share),
        mixed_grad[:, :q_cols],
        mixed_grad[:, q_cols : q_cols + kv_cols],
        mixed_grad[:, q_cols + kv_cols :],
        out_weight_grad,
        small[2 * width : 2 * width + HEAD_SIZE],
        small[2 * width + HEAD_SIZE :],
        take(small, width + first, share),
        gate_grad,
        up_grad,
        down_grad,
    )


def solution(mesh):
    return jax.shard_map(
        per_device,
        mesh=mesh,
        in_specs=(
            P("fsdp", "ctx", None),
            P("fsdp", None),
            P("fsdp", "ctx"),
            P("fsdp"),
            P("fsdp", "tp"),
            P("fsdp", "tp"),
            P("fsdp", "tp"),
            P("fsdp", "tp"),
            P(),
            P(),
            P("fsdp"),
            P("fsdp", "tp"),
            P("fsdp", "tp"),
            P("fsdp", "tp"),
            P("fsdp", "ctx", None),
        ),
        out_specs=(
            P("fsdp", "ctx", None),
            P("fsdp", "ctx", None),
            P("fsdp"),
            P("fsdp", "tp"),
            P("fsdp", "tp"),
            P("fsdp", "tp"),
            P("fsdp", "tp"),
            P(),
            P(),
            P("fsdp"),
            P("fsdp", "tp"),
            P("fsdp", "tp"),
            P("fsdp", "tp"),
        ),
        check_vma=False,
    )
```

```python
import jax
import jax.numpy as jnp
from jax import lax
from jax.sharding import PartitionSpec as P

HEAD_SIZE = 64
MAX_DOC = 1024


eps = 1e-05
theta = 1000000.0


def ring(count, step):
    return [(i, (i + step) % count) for i in range(count)]


def swap(count):
    return [(i, i ^ 1) for i in range(count)]


def rounded(value):
    return lax.reduce_precision(value, 8, 7).astype(jnp.bfloat16)


def take(value, start, size, axis=0):
    return lax.dynamic_slice_in_dim(value, start, size, axis)


def put(whole, part, start, axis=0):
    return lax.dynamic_update_slice_in_dim(whole, part, start, axis)


def gather(part, name, axis=0):
    count, me, size = lax.axis_size(name), lax.axis_index(name), part.shape[axis]
    shape = list(part.shape)
    shape[axis] = count * size
    whole = put(jnp.zeros(shape, part.dtype), part, me * size, axis)
    for k in range(1, count):
        got = lax.ppermute(part, name, ring(count, k))
        whole = put(whole, got, ((me - k) % count) * size, axis)
    return whole


def paired(count):
    return count % 2 == 0


def fetch_half(part):
    ctx, count = lax.axis_size("ctx"), lax.axis_size("fsdp")
    size = part.shape[0]
    half = size // 2 if paired(ctx) and size % 32 == 0 else size
    mine = take(part, (lax.axis_index("ctx") % 2) * half if half < size else 0, half)
    return [lax.ppermute(mine, "fsdp", ring(count, k)) for k in range(1, count)]


def join_halves(part, halves):
    ctx, count, me = lax.axis_size("ctx"), lax.axis_size("fsdp"), lax.axis_index("fsdp")
    size, side = part.shape[0], lax.axis_index("ctx") % 2
    whole = put(jnp.zeros((count * size, part.shape[1]), part.dtype), part, me * size)
    for k in range(1, count):
        got, start = halves[k - 1], ((me - k) % count) * size
        if got.shape[0] == size:
            whole = put(whole, got, start)
            continue
        other = lax.ppermute(got, "ctx", swap(ctx))
        whole = put(whole, got, start + side * (size // 2))
        whole = put(whole, other, start + (1 - side) * (size // 2))
    return whole


def hold(*values):
    return lax.optimization_barrier(values)


def all_sum(value):
    for name in ("tp", "fsdp", "ctx"):
        value = jnp.sum(gather(value[None], name), axis=0)
    return value


def scatter_rows(part, name):
    count, me = lax.axis_size(name), lax.axis_index(name)
    size = part.shape[0] // count
    total = take(part, me * size, size).astype(jnp.float32)
    for k in range(1, count):
        block = take(part, ((me + k) % count) * size, size)
        total = total + lax.ppermute(block, name, ring(count, k)).astype(jnp.float32)
    return total


def split_of(size):
    return 2 if paired(lax.axis_size("ctx")) and size % 32 == 0 else 1


def reduce_pair(grad):
    count, ctx = lax.axis_size("fsdp"), lax.axis_size("ctx")
    size = grad.shape[0] // count
    split = split_of(size)
    side = lax.axis_index("ctx") % split
    blocks = grad.reshape(count, split, size // split, grad.shape[1])
    mine = take(blocks, side, 1, 1)[:, 0]
    if split == 2:
        away = take(blocks, 1 - side, 1, 1)[:, 0]
        got = lax.ppermute(away, "ctx", swap(ctx))
        mine = (mine.astype(jnp.float32) + got.astype(jnp.float32)).astype(jnp.bfloat16)
    return mine


def reduce_fsdp(mine):
    count, me = lax.axis_size("fsdp"), lax.axis_index("fsdp")
    total = take(mine, me, 1)[0].astype(jnp.float32)
    for k in range(1, count):
        block = take(mine, (me + k) % count, 1)[0]
        total = total + lax.ppermute(block, "fsdp", ring(count, k)).astype(jnp.float32)
    return rounded(total)


def reduce_far(sent, size):
    ctx, place = lax.axis_size("ctx"), lax.axis_index("ctx")
    split = split_of(size)
    side, far = place % split, ctx // split
    total = sent.astype(jnp.float32)
    if far == 2:
        total = total + lax.ppermute(sent, "ctx", ring(ctx, split)).astype(jnp.float32)
    elif far > 2:
        whole = put(jnp.zeros((far,) + sent.shape, jnp.bfloat16), sent[None], place // split)
        for k in range(1, far):
            got = lax.ppermute(sent, "ctx", ring(ctx, k * split))
            whole = put(whole, got[None], (place // split - k) % far)
        total = jnp.sum(whole.astype(jnp.float32), axis=0)
    if split == 1:
        return total
    sent = rounded(total)
    got = lax.ppermute(sent, "ctx", swap(ctx))
    low = jnp.where(side == 0, sent, got)
    high = jnp.where(side == 0, got, sent)
    return jnp.concatenate([low, high], axis=0).astype(jnp.float32)


def reduce_grad(grad):
    return reduce_far(reduce_fsdp(reduce_pair(grad)), grad.shape[0] // lax.axis_size("fsdp"))


def dot(left, right, dims=((1,), (0,)), out=jnp.float32):
    return lax.dot_general(left, right, (dims, ((), ())), preferred_element_type=jnp.float32).astype(out)


def rms_scale(value_rows):
    return lax.rsqrt(jnp.mean(value_rows * value_rows, axis=-1, keepdims=True) + eps)


def norm_back(value_rows, scale, gain, grad_out):
    normed = value_rows * scale
    grad_normed = grad_out * gain
    grad_values = scale * (
        grad_normed - normed * jnp.mean(grad_normed * normed, axis=-1, keepdims=True)
    )
    return (grad_values, grad_out * normed)


def rope_tables(positions, width):
    half = width // 2
    freq = theta ** (-(jnp.arange(half, dtype=jnp.float32) * 2.0 / width))
    angle = positions.astype(jnp.float32)[:, None] * freq[None, :]
    angle = jnp.concatenate([angle, angle], axis=-1)
    return (jnp.cos(angle)[:, None, :], jnp.sin(angle)[:, None, :])


def rotate(value_rows, cosine, sine):
    half = value_rows.shape[-1] // 2
    turned = jnp.concatenate([-value_rows[..., half:], value_rows[..., :half]], axis=-1)
    return value_rows * cosine + turned * sine


def rotate_back(grads, cosine, sine):
    half = grads.shape[-1] // 2
    scaled = grads * sine
    turned = jnp.concatenate([scaled[..., half:], -scaled[..., :half]], axis=-1)
    return grads * cosine + turned


def per_device(
    block_input,
    segment_ids,
    positions,
    attn_gain,
    query_weight,
    key_matrix,
    value_matrix,
    output_weight,
    query_gain,
    key_gain,
    ffn_gain,
    gate_weight,
    up_weight,
    down_weight,
    out_grad,
):
    f32 = jnp.float32
    bf16 = jnp.bfloat16
    inputs = block_input[0]
    grad_out = out_grad[0]
    rows = inputs.shape[0]
    width = inputs.shape[1]
    seg_all = segment_ids[0]
    ctx, place = lax.axis_size("ctx"), lax.axis_index("ctx")
    tp, rank = lax.axis_size("tp"), lax.axis_index("tp")
    own = rows // tp
    q_cols, kv_cols = query_weight.shape[1], key_matrix.shape[1]
    q_count, kv_count = q_cols // HEAD_SIZE, kv_cols // HEAD_SIZE
    groups = q_count // kv_count

    gains = gather(jnp.stack([attn_gain, ffn_gain]), "fsdp", 1).astype(f32)
    gain_one, gain_two = gains[0], gains[1]
    w_attn = gather(
        jnp.concatenate([query_weight, key_matrix, value_matrix, output_weight], axis=1), "fsdp"
    )
    w_in, w_out = w_attn[:, : q_cols + 2 * kv_cols], w_attn[:, q_cols + 2 * kv_cols :]
    ffn_weights = (gate_weight, up_weight, down_weight)
    w_in, *held = hold(w_in, *ffn_weights)
    halves = [fetch_half(part) for part in held]

    inputs_f = inputs.astype(f32)
    scale_one = rms_scale(inputs_f)
    normed_one = (inputs_f * scale_one * gain_one).astype(bf16)
    cosine, sine = rope_tables(positions[0], HEAD_SIZE)
    mixed = dot(normed_one, w_in)
    query_raw = mixed[:, :q_cols].reshape(rows, q_count, HEAD_SIZE)
    key_raw = mixed[:, q_cols : q_cols + kv_cols].reshape(rows, kv_count, HEAD_SIZE)
    values = mixed[:, q_cols + kv_cols :].astype(bf16)
    query_gain_f = query_gain.astype(f32)
    key_gain_f = key_gain.astype(f32)
    query_scale = rms_scale(query_raw)
    key_scale = rms_scale(key_raw)
    factor = HEAD_SIZE ** (-0.5)
    query = rotate(query_raw * query_scale * query_gain_f, cosine, sine).astype(bf16)
    query = (query * factor).astype(bf16).reshape(rows, kv_count, groups, HEAD_SIZE)
    key = rotate(key_raw * key_scale * key_gain_f, cosine, sine).astype(bf16)
    both = jnp.concatenate([key.reshape(rows, kv_cols), values], axis=1)

    near = min(ctx, 1 + (MAX_DOC - 1 + rows - 1) // rows)
    both_parts, seg_parts, index_parts = [both], [], []
    step = jnp.arange(rows, dtype=jnp.int32)
    for k in range(near):
        if k:
            both_parts.append(lax.ppermute(both, "ctx", ring(ctx, k)))
        start = ((place - k) % ctx) * rows
        seg_parts.append(take(seg_all, start, rows))
        index_parts.append(start + step)
    both_near = jnp.concatenate(both_parts, axis=0)
    seg_near = jnp.concatenate(seg_parts)
    index_near = jnp.concatenate(index_parts)
    mask = (seg_parts[0][:, None] == seg_near[None, :]) & (
        index_near[None, :] <= index_parts[0][:, None]
    )
    keys_near = both_near[:, :kv_cols].reshape(-1, kv_count, HEAD_SIZE)
    values_near = both_near[:, kv_cols:].reshape(-1, kv_count, HEAD_SIZE)

    scores = jnp.einsum("bkgd,skd->kgbs", query, keys_near, preferred_element_type=f32)
    scores = jnp.where(mask[None, None], scores, -1e30)
    top = jnp.max(scores, axis=-1, keepdims=True)
    total = jnp.sum(jnp.exp(scores - top), axis=-1, keepdims=True)
    probs = jnp.exp(scores - (top + jnp.log(total))).astype(bf16)
    heads_out = jnp.einsum("kgbs,skd->bkgd", probs, values_near, preferred_element_type=f32)
    heads_out = heads_out.astype(bf16)
    heads_rows = heads_out.reshape(rows, q_cols)

    def own_rows(value):
        return take(value, rank * own, own)

    heads_rows, halves = hold(heads_rows, halves)
    attn_part = dot(heads_rows, w_out, ((1,), (1,)), bf16)
    w_gate, w_up, w_down = [join_halves(w, got) for w, got in zip(ffn_weights, halves)]
    residual = own_rows(inputs).astype(f32) + scatter_rows(attn_part, "tp")
    scale_two = rms_scale(residual)
    normed_two = gather((residual * scale_two * gain_two).astype(bf16), "tp")
    gate = dot(normed_two, w_gate)
    up = dot(normed_two, w_up)
    grad_act = dot(grad_out, w_down)
    sigmoid = jax.nn.sigmoid(gate)
    silu_gate = gate * sigmoid
    activation = (silu_gate * up).astype(bf16)
    grad_gate = (grad_act * up * sigmoid * (1.0 + gate * (1.0 - sigmoid))).astype(bf16)
    grad_up = (grad_act * silu_gate).astype(bf16)

    normed_two_part = (
        dot(grad_gate, w_gate, ((1,), (1,))) + dot(grad_up, w_up, ((1,), (1,)))
    ).astype(bf16)
    normed_two_part, activation, grad_gate, grad_up = hold(
        normed_two_part, activation, grad_gate, grad_up
    )
    pairs = [
        reduce_pair(dot(grad_out, activation, ((0,), (0,)), bf16)),
        reduce_pair(dot(normed_two, grad_gate, ((0,), (0,)), bf16)),
        reduce_pair(dot(normed_two, grad_up, ((0,), (0,)), bf16)),
    ]
    normed_two_grad = scatter_rows(normed_two_part, "tp")
    normed_two_grad, pairs = hold(normed_two_grad, pairs)
    shares = [reduce_fsdp(part) for part in pairs]
    residual_back, ffn_terms = norm_back(residual, scale_two, gain_two, normed_two_grad)
    residual_grad = own_rows(grad_out).astype(f32) + residual_back
    residual_bf = gather(residual_grad.astype(bf16), "tp")
    residual_bf, activation = hold(residual_bf, activation)

    ffn_part = dot(activation, w_down, ((1,), (1,)), bf16)
    output = gather((residual + scatter_rows(ffn_part, "tp")).astype(bf16), "tp")
    heads_grad = dot(residual_bf, w_out, ((1,), (0,)), bf16)
    out_weight_grad = reduce_grad(dot(residual_bf, heads_rows, ((0,), (0,)), bf16))
    heads_grad = heads_grad.reshape(heads_out.shape)
    values_grad_near = jnp.einsum("kgbs,bkgd->skd", probs, heads_grad, preferred_element_type=f32)
    grad_probs = jnp.einsum("bkgd,skd->kgbs", heads_grad, values_near, preferred_element_type=f32)
    delta = jnp.sum(heads_grad.astype(f32) * heads_out.astype(f32), axis=-1)
    delta = jnp.transpose(delta, (1, 2, 0))[..., None]
    grad_scores = (probs.astype(f32) * (grad_probs - delta)).astype(bf16)
    keys_grad_near = jnp.einsum("kgbs,bkgd->skd", grad_scores, query, preferred_element_type=f32)
    query_grad = (
        jnp.einsum("kgbs,skd->bkgd", grad_scores, keys_near, preferred_element_type=f32) * factor
    )

    both_grad = jnp.concatenate(
        [keys_grad_near.reshape(-1, kv_cols), values_grad_near.reshape(-1, kv_cols)], axis=1
    )
    both_sum = both_grad[:rows]
    for k in range(1, near):
        block = both_grad[k * rows : (k + 1) * rows].astype(bf16)
        both_sum = both_sum + lax.ppermute(block, "ctx", ring(ctx, -k)).astype(f32)
    keys_grad = both_sum[:, :kv_cols].reshape(rows, kv_count, HEAD_SIZE)
    values_bf = both_sum[:, kv_cols:].astype(bf16)

    query_pre, query_terms = norm_back(
        query_raw,
        query_scale,
        query_gain_f,
        rotate_back(query_grad.reshape(query_raw.shape), cosine, sine),
    )
    key_pre, key_terms = norm_back(
        key_raw, key_scale, key_gain_f, rotate_back(keys_grad, cosine, sine)
    )
    mixed_pre = jnp.concatenate(
        [
            query_pre.reshape(rows, q_cols).astype(bf16),
            key_pre.reshape(rows, kv_cols).astype(bf16),
            values_bf,
        ],
        axis=1,
    )
    normed_one_part = dot(mixed_pre, w_in, ((1,), (1,)), bf16)
    normed_one_part, shares = hold(normed_one_part, shares)
    share = attn_gain.shape[0]
    down_grad, gate_grad, up_grad = [reduce_far(part, share) for part in shares]
    normed_one_grad = scatter_rows(normed_one_part, "tp")
    input_back, attn_terms = norm_back(
        own_rows(inputs).astype(f32), own_rows(scale_one), gain_one, normed_one_grad
    )
    input_grad = gather(rounded(residual_grad + input_back), "tp").astype(f32)
    mixed_grad = reduce_grad(dot(normed_one, mixed_pre, ((0,), (0,)), bf16))

    small = all_sum(
        jnp.concatenate(
            [
                jnp.sum(attn_terms, axis=0),
                jnp.sum(ffn_terms, axis=0),
                jnp.sum(query_terms, axis=(0, 1)),
                jnp.sum(key_terms, axis=(0, 1)),
            ]
        )
    )
    first = lax.axis_index("fsdp") * share
    return (
        output[None],
        input_grad[None],
        take(small, first, share),
        mixed_grad[:, :q_cols],
        mixed_grad[:, q_cols : q_cols + kv_cols],
        mixed_grad[:, q_cols + kv_cols :],
        out_weight_grad,
        small[2 * width : 2 * width + HEAD_SIZE],
        small[2 * width + HEAD_SIZE :],
        take(small, width + first, share),
        gate_grad,
        up_grad,
        down_grad,
    )


def solution(mesh):
    return jax.shard_map(
        per_device,
        mesh=mesh,
        in_specs=(
            P("fsdp", "ctx", None),
            P("fsdp", None),
            P("fsdp", "ctx"),
            P("fsdp"),
            P("fsdp", "tp"),
            P("fsdp", "tp"),
            P("fsdp", "tp"),
            P("fsdp", "tp"),
            P(),
            P(),
            P("fsdp"),
            P("fsdp", "tp"),
            P("fsdp", "tp"),
            P("fsdp", "tp"),
            P("fsdp", "ctx", None),
        ),
        out_specs=(
            P("fsdp", "ctx", None),
            P("fsdp", "ctx", None),
            P("fsdp"),
            P("fsdp", "tp"),
            P("fsdp", "tp"),
            P("fsdp", "tp"),
            P("fsdp", "tp"),
            P(),
            P(),
            P("fsdp"),
            P("fsdp", "tp"),
            P("fsdp", "tp"),
            P("fsdp", "tp"),
        ),
        check_vma=False,
    )
```

```python
import jax
import jax.numpy as jnp
from jax import lax
from jax.sharding import PartitionSpec as P

HEAD_SIZE = 64
MAX_DOC = 1024


eps = 1e-05
theta = 1000000.0


def ring(count, step):
    return [(i, (i + step) % count) for i in range(count)]


def swap(count):
    return [(i, i ^ 1) for i in range(count)]


def rounded(value):
    return lax.reduce_precision(value, 8, 7).astype(jnp.bfloat16)


def take(value, start, size, axis=0):
    return lax.dynamic_slice_in_dim(value, start, size, axis)


def put(whole, part, start, axis=0):
    return lax.dynamic_update_slice_in_dim(whole, part, start, axis)


def gather(part, name, axis=0):
    count, me, size = lax.axis_size(name), lax.axis_index(name), part.shape[axis]
    shape = list(part.shape)
    shape[axis] = count * size
    whole = put(jnp.zeros(shape, part.dtype), part, me * size, axis)
    for k in range(1, count):
        got = lax.ppermute(part, name, ring(count, k))
        whole = put(whole, got, ((me - k) % count) * size, axis)
    return whole


def paired(count):
    return count % 2 == 0


def fetch_half(part):
    ctx, count = lax.axis_size("ctx"), lax.axis_size("fsdp")
    size = part.shape[0]
    half = size // 2 if paired(ctx) and size % 32 == 0 else size
    mine = take(part, (lax.axis_index("ctx") % 2) * half if half < size else 0, half)
    return [lax.ppermute(mine, "fsdp", ring(count, k)) for k in range(1, count)]


def join_halves(part, halves):
    ctx, count, me = lax.axis_size("ctx"), lax.axis_size("fsdp"), lax.axis_index("fsdp")
    size, side = part.shape[0], lax.axis_index("ctx") % 2
    whole = put(jnp.zeros((count * size, part.shape[1]), part.dtype), part, me * size)
    for k in range(1, count):
        got, start = halves[k - 1], ((me - k) % count) * size
        if got.shape[0] == size:
            whole = put(whole, got, start)
            continue
        other = lax.ppermute(got, "ctx", swap(ctx))
        whole = put(whole, got, start + side * (size // 2))
        whole = put(whole, other, start + (1 - side) * (size // 2))
    return whole


def hold(*values):
    return lax.optimization_barrier(values)


def all_sum(value):
    for name in ("tp", "fsdp", "ctx"):
        value = jnp.sum(gather(value[None], name), axis=0)
    return value


def scatter_rows(part, name):
    count, me = lax.axis_size(name), lax.axis_index(name)
    size = part.shape[0] // count
    total = take(part, me * size, size).astype(jnp.float32)
    for k in range(1, count):
        block = take(part, ((me + k) % count) * size, size)
        total = total + lax.ppermute(block, name, ring(count, k)).astype(jnp.float32)
    return total


def split_of(size):
    return 2 if paired(lax.axis_size("ctx")) and size % 32 == 0 else 1


def reduce_pair(grad):
    count, ctx = lax.axis_size("fsdp"), lax.axis_size("ctx")
    size = grad.shape[0] // count
    split = split_of(size)
    side = lax.axis_index("ctx") % split
    blocks = grad.reshape(count, split, size // split, grad.shape[1])
    mine = take(blocks, side, 1, 1)[:, 0]
    if split == 2:
        away = take(blocks, 1 - side, 1, 1)[:, 0]
        got = lax.ppermute(away, "ctx", swap(ctx))
        mine = (mine.astype(jnp.float32) + got.astype(jnp.float32)).astype(jnp.bfloat16)
    return mine


def reduce_fsdp(mine):
    count, me = lax.axis_size("fsdp"), lax.axis_index("fsdp")
    total = take(mine, me, 1)[0].astype(jnp.float32)
    for k in range(1, count):
        block = take(mine, (me + k) % count, 1)[0]
        total = total + lax.ppermute(block, "fsdp", ring(count, k)).astype(jnp.float32)
    return rounded(total)


def reduce_far(sent, size):
    ctx, place = lax.axis_size("ctx"), lax.axis_index("ctx")
    split = split_of(size)
    side, far = place % split, ctx // split
    total = sent.astype(jnp.float32)
    if far == 2:
        total = total + lax.ppermute(sent, "ctx", ring(ctx, split)).astype(jnp.float32)
    elif far > 2:
        whole = put(jnp.zeros((far,) + sent.shape, jnp.bfloat16), sent[None], place // split)
        for k in range(1, far):
            got = lax.ppermute(sent, "ctx", ring(ctx, k * split))
            whole = put(whole, got[None], (place // split - k) % far)
        total = jnp.sum(whole.astype(jnp.float32), axis=0)
    if split == 1:
        return total
    sent = rounded(total)
    got = lax.ppermute(sent, "ctx", swap(ctx))
    low = jnp.where(side == 0, sent, got)
    high = jnp.where(side == 0, got, sent)
    return jnp.concatenate([low, high], axis=0).astype(jnp.float32)


def reduce_grad(grad):
    return reduce_far(reduce_fsdp(reduce_pair(grad)), grad.shape[0] // lax.axis_size("fsdp"))


def dot(left, right, dims=((1,), (0,)), out=jnp.float32):
    return lax.dot_general(left, right, (dims, ((), ())), preferred_element_type=jnp.float32).astype(out)


def rms_scale(value_rows):
    return lax.rsqrt(jnp.mean(value_rows * value_rows, axis=-1, keepdims=True) + eps)


def norm_back(value_rows, scale, gain, grad_out):
    normed = value_rows * scale
    grad_normed = grad_out * gain
    grad_values = scale * (
        grad_normed - normed * jnp.mean(grad_normed * normed, axis=-1, keepdims=True)
    )
    return (grad_values, grad_out * normed)


def rope_tables(positions, width):
    half = width // 2
    freq = theta ** (-(jnp.arange(half, dtype=jnp.float32) * 2.0 / width))
    angle = positions.astype(jnp.float32)[:, None] * freq[None, :]
    angle = jnp.concatenate([angle, angle], axis=-1)
    return (jnp.cos(angle)[:, None, :], jnp.sin(angle)[:, None, :])


def rotate(value_rows, cosine, sine):
    half = value_rows.shape[-1] // 2
    turned = jnp.concatenate([-value_rows[..., half:], value_rows[..., :half]], axis=-1)
    return value_rows * cosine + turned * sine


def rotate_back(grads, cosine, sine):
    half = grads.shape[-1] // 2
    scaled = grads * sine
    turned = jnp.concatenate([scaled[..., half:], -scaled[..., :half]], axis=-1)
    return grads * cosine + turned


def per_device(
    block_input,
    segment_ids,
    positions,
    attn_gain,
    query_weight,
    key_matrix,
    value_matrix,
    output_weight,
    query_gain,
    key_gain,
    ffn_gain,
    gate_weight,
    up_weight,
    down_weight,
    out_grad,
):
    f32 = jnp.float32
    bf16 = jnp.bfloat16
    inputs = block_input[0]
    grad_out = out_grad[0]
    rows = inputs.shape[0]
    width = inputs.shape[1]
    seg_all = segment_ids[0]
    ctx, place = lax.axis_size("ctx"), lax.axis_index("ctx")
    tp, rank = lax.axis_size("tp"), lax.axis_index("tp")
    own = rows // tp
    q_cols, kv_cols = query_weight.shape[1], key_matrix.shape[1]
    q_count, kv_count = q_cols // HEAD_SIZE, kv_cols // HEAD_SIZE
    groups = q_count // kv_count

    gains = gather(jnp.stack([attn_gain, ffn_gain]), "fsdp", 1).astype(f32)
    gain_one, gain_two = gains[0], gains[1]
    w_attn = gather(
        jnp.concatenate([query_weight, key_matrix, value_matrix, output_weight], axis=1), "fsdp"
    )
    w_in, w_out = w_attn[:, : q_cols + 2 * kv_cols], w_attn[:, q_cols + 2 * kv_cols :]
    ffn_weights = (gate_weight, up_weight, down_weight)
    w_in, *held = hold(w_in, *ffn_weights)
    halves = [fetch_half(part) for part in held]

    inputs_f = inputs.astype(f32)
    scale_one = rms_scale(inputs_f)
    normed_one = (inputs_f * scale_one * gain_one).astype(bf16)
    cosine, sine = rope_tables(positions[0], HEAD_SIZE)
    mixed = dot(normed_one, w_in)
    query_raw = mixed[:, :q_cols].reshape(rows, q_count, HEAD_SIZE)
    key_raw = mixed[:, q_cols : q_cols + kv_cols].reshape(rows, kv_count, HEAD_SIZE)
    values = mixed[:, q_cols + kv_cols :].astype(bf16)
    query_gain_f = query_gain.astype(f32)
    key_gain_f = key_gain.astype(f32)
    query_scale = rms_scale(query_raw)
    key_scale = rms_scale(key_raw)
    factor = HEAD_SIZE ** (-0.5)
    query = rotate(query_raw * query_scale * query_gain_f, cosine, sine).astype(bf16)
    query = (query * factor).astype(bf16).reshape(rows, kv_count, groups, HEAD_SIZE)
    key = rotate(key_raw * key_scale * key_gain_f, cosine, sine).astype(bf16)
    both = jnp.concatenate([key.reshape(rows, kv_cols), values], axis=1)

    near = min(ctx, 1 + (MAX_DOC - 1 + rows - 1) // rows)
    both_parts, seg_parts, index_parts = [both], [], []
    step = jnp.arange(rows, dtype=jnp.int32)
    for k in range(near):
        if k:
            both_parts.append(lax.ppermute(both, "ctx", ring(ctx, k)))
        start = ((place - k) % ctx) * rows
        seg_parts.append(take(seg_all, start, rows))
        index_parts.append(start + step)
    both_near = jnp.concatenate(both_parts, axis=0)
    seg_near = jnp.concatenate(seg_parts)
    index_near = jnp.concatenate(index_parts)
    mask = (seg_parts[0][:, None] == seg_near[None, :]) & (
        index_near[None, :] <= index_parts[0][:, None]
    )
    keys_near = both_near[:, :kv_cols].reshape(-1, kv_count, HEAD_SIZE)
    values_near = both_near[:, kv_cols:].reshape(-1, kv_count, HEAD_SIZE)

    scores = jnp.einsum("bkgd,skd->kgbs", query, keys_near, preferred_element_type=f32)
    scores = jnp.where(mask[None, None], scores, -1e30)
    top = jnp.max(scores, axis=-1, keepdims=True)
    total = jnp.sum(jnp.exp(scores - top), axis=-1, keepdims=True)
    probs = jnp.exp(scores - (top + jnp.log(total))).astype(bf16)
    heads_out = jnp.einsum("kgbs,skd->bkgd", probs, values_near, preferred_element_type=f32)
    heads_out = heads_out.astype(bf16)
    heads_rows = heads_out.reshape(rows, q_cols)

    def own_rows(value):
        return take(value, rank * own, own)

    heads_rows, halves = hold(heads_rows, halves)
    attn_part = dot(heads_rows, w_out, ((1,), (1,)), bf16)
    w_gate, w_up, w_down = [join_halves(w, got) for w, got in zip(ffn_weights, halves)]
    residual = own_rows(inputs).astype(f32) + scatter_rows(attn_part, "tp")
    scale_two = rms_scale(residual)
    normed_two = gather((residual * scale_two * gain_two).astype(bf16), "tp")
    gate = dot(normed_two, w_gate)
    up = dot(normed_two, w_up)
    grad_act = dot(grad_out, w_down)
    sigmoid = jax.nn.sigmoid(gate)
    silu_gate = gate * sigmoid
    activation = (silu_gate * up).astype(bf16)
    grad_gate = (grad_act * up * sigmoid * (1.0 + gate * (1.0 - sigmoid))).astype(bf16)
    grad_up = (grad_act * silu_gate).astype(bf16)

    normed_two_part = (
        dot(grad_gate, w_gate, ((1,), (1,))) + dot(grad_up, w_up, ((1,), (1,)))
    ).astype(bf16)
    normed_two_part, activation, grad_gate, grad_up = hold(
        normed_two_part, activation, grad_gate, grad_up
    )
    pairs = [
        reduce_pair(dot(grad_out, activation, ((0,), (0,)), bf16)),
        reduce_pair(dot(normed_two, grad_gate, ((0,), (0,)), bf16)),
        reduce_pair(dot(normed_two, grad_up, ((0,), (0,)), bf16)),
    ]
    normed_two_grad = scatter_rows(normed_two_part, "tp")
    normed_two_grad, pairs = hold(normed_two_grad, pairs)
    shares = [reduce_fsdp(part) for part in pairs]
    residual_back, ffn_terms = norm_back(residual, scale_two, gain_two, normed_two_grad)
    residual_grad = own_rows(grad_out).astype(f32) + residual_back
    residual_bf = gather(residual_grad.astype(bf16), "tp")
    residual_bf, activation = hold(residual_bf, activation)

    ffn_part = dot(activation, w_down, ((1,), (1,)), bf16)
    output = gather((residual + scatter_rows(ffn_part, "tp")).astype(bf16), "tp")
    heads_grad = dot(residual_bf, w_out, ((1,), (0,)), bf16)
    out_share = reduce_fsdp(reduce_pair(dot(residual_bf, heads_rows, ((0,), (0,)), bf16)))
    heads_grad = heads_grad.reshape(heads_out.shape)
    values_grad_near = jnp.einsum("kgbs,bkgd->skd", probs, heads_grad, preferred_element_type=f32)
    grad_probs = jnp.einsum("bkgd,skd->kgbs", heads_grad, values_near, preferred_element_type=f32)
    delta = jnp.sum(heads_grad.astype(f32) * heads_out.astype(f32), axis=-1)
    delta = jnp.transpose(delta, (1, 2, 0))[..., None]
    grad_scores = (probs.astype(f32) * (grad_probs - delta)).astype(bf16)
    keys_grad_near = jnp.einsum("kgbs,bkgd->skd", grad_scores, query, preferred_element_type=f32)
    query_grad = (
        jnp.einsum("kgbs,skd->bkgd", grad_scores, keys_near, preferred_element_type=f32) * factor
    )

    both_grad = jnp.concatenate(
        [keys_grad_near.reshape(-1, kv_cols), values_grad_near.reshape(-1, kv_cols)], axis=1
    )
    both_sum = both_grad[:rows]
    for k in range(1, near):
        block = both_grad[k * rows : (k + 1) * rows].astype(bf16)
        both_sum = both_sum + lax.ppermute(block, "ctx", ring(ctx, -k)).astype(f32)
    keys_grad = both_sum[:, :kv_cols].reshape(rows, kv_count, HEAD_SIZE)
    values_bf = both_sum[:, kv_cols:].astype(bf16)

    query_pre, query_terms = norm_back(
        query_raw,
        query_scale,
        query_gain_f,
        rotate_back(query_grad.reshape(query_raw.shape), cosine, sine),
    )
    key_pre, key_terms = norm_back(
        key_raw, key_scale, key_gain_f, rotate_back(keys_grad, cosine, sine)
    )
    mixed_pre = jnp.concatenate(
        [
            query_pre.reshape(rows, q_cols).astype(bf16),
            key_pre.reshape(rows, kv_cols).astype(bf16),
            values_bf,
        ],
        axis=1,
    )
    normed_one_part = dot(mixed_pre, w_in, ((1,), (1,)), bf16)
    normed_one_part, shares = hold(normed_one_part, shares)
    share = attn_gain.shape[0]
    down_grad, gate_grad, up_grad = [reduce_far(part, share) for part in shares]
    normed_one_grad = scatter_rows(normed_one_part, "tp")
    normed_one_grad, out_share = hold(normed_one_grad, out_share)
    out_weight_grad = reduce_far(out_share, share)
    input_back, attn_terms = norm_back(
        own_rows(inputs).astype(f32), own_rows(scale_one), gain_one, normed_one_grad
    )
    input_grad = gather(rounded(residual_grad + input_back), "tp").astype(f32)
    mixed_grad = reduce_grad(dot(normed_one, mixed_pre, ((0,), (0,)), bf16))

    small = all_sum(
        jnp.concatenate(
            [
                jnp.sum(attn_terms, axis=0),
                jnp.sum(ffn_terms, axis=0),
                jnp.sum(query_terms, axis=(0, 1)),
                jnp.sum(key_terms, axis=(0, 1)),
            ]
        )
    )
    first = lax.axis_index("fsdp") * share
    return (
        output[None],
        input_grad[None],
        take(small, first, share),
        mixed_grad[:, :q_cols],
        mixed_grad[:, q_cols : q_cols + kv_cols],
        mixed_grad[:, q_cols + kv_cols :],
        out_weight_grad,
        small[2 * width : 2 * width + HEAD_SIZE],
        small[2 * width + HEAD_SIZE :],
        take(small, width + first, share),
        gate_grad,
        up_grad,
        down_grad,
    )


def solution(mesh):
    return jax.shard_map(
        per_device,
        mesh=mesh,
        in_specs=(
            P("fsdp", "ctx", None),
            P("fsdp", None),
            P("fsdp", "ctx"),
            P("fsdp"),
            P("fsdp", "tp"),
            P("fsdp", "tp"),
            P("fsdp", "tp"),
            P("fsdp", "tp"),
            P(),
            P(),
            P("fsdp"),
            P("fsdp", "tp"),
            P("fsdp", "tp"),
            P("fsdp", "tp"),
            P("fsdp", "ctx", None),
        ),
        out_specs=(
            P("fsdp", "ctx", None),
            P("fsdp", "ctx", None),
            P("fsdp"),
            P("fsdp", "tp"),
            P("fsdp", "tp"),
            P("fsdp", "tp"),
            P("fsdp", "tp"),
            P(),
            P(),
            P("fsdp"),
            P("fsdp", "tp"),
            P("fsdp", "tp"),
            P("fsdp", "tp"),
        ),
        check_vma=False,
    )
```
